128 devices in a mesh: obs: 4 (over z_hi, core), par: 32 (over y, x, z_lo).
Axes of the slice: x: 4, y: 4, z: 4 (z_hi: 2, z_lo: 2; z = z_hi * 2 + z_lo), core: 2. Of those that a mesh axis runs over, the one named last changes fastest.
Arguments:
- jacobian: bfloat16 [3072, 16384], P(('obs', 'par')), may hold values from -0.109375 to 0.109375
- obs_weights: float32 [3072], replicated, may hold values from 0.1 to 10
- time_to_obs: int32 [3072], P(('obs', 'par')), may hold values from 0 to 3071, each once
Outputs:
- normal_matrix: float32 [16384, 16384], P('obs', 'par')
The draws below stay inside these ranges and needn't reach their ends.
Inputs may be any that keep to these rules, and one draw needn't show every extreme that they name: `time_to_obs`: each observation index appears exactly once.
All inputs are finite; a program needn't handle non-finite values.
Results may differ from the reference program's by a relative error of at most 0.0039.
Values may be sent and summed in bfloat16 or wider, within the bound.
No kernel may reach another device: no remote copies, remote signals or barrier semaphores. Data moves between devices by JAX's collectives and lax.ppermute only.
A program may use at most 128 MiB of HBM per device.

```python
import math
import jax
import jax.numpy as jnp

PARAMS = 16384
ROWS = 3072


def block_scale(own_key, dims, split, low, top_value):
    level, own = 1.0, jax.random.fold_in(own_key, 6)
    for position, shards_of in split:
        steps = jnp.exp(jax.random.uniform(jax.random.fold_in(own, position), (shards_of,), jnp.float32, low / len(split), top_value / len(split)))
        level = level * jnp.repeat(steps, dims[position] // shards_of).reshape([-1 if axis == position else 1 for axis in range(len(dims))])
    return level


def centred(rng, dims, spread, bound, cuts=(), dtype=jnp.bfloat16):
    result = jax.random.normal(rng, dims, jnp.float32) * spread
    if len(cuts) > 0:
        result = block_scale(rng, dims, cuts, -0.22, 0.18) * result
    return jnp.clip(result, min=-bound, max=bound).astype(dtype)


def setup_inputs(seed: int = 0) -> dict:
    arg_keys = jax.random.split(jax.random.key(seed), 4)
    return {
        "jacobian": centred(arg_keys[0], (ROWS, PARAMS), ROWS ** -0.5, 0.109375, ((0, 128),)),
        "obs_weights": jnp.clip(jnp.exp(jax.random.uniform(arg_keys[1], (ROWS,), jnp.float32, math.log(0.1), math.log(10.0))), 0.1, 10.0),
        "time_to_obs": jax.random.permutation(arg_keys[2], ROWS).astype(jnp.int32),
    }


def reference(jacobian, obs_weights, time_to_obs):
    row_weight = obs_weights[time_to_obs]
    scaled = (jnp.sqrt(row_weight)[:, None] * jacobian.astype(jnp.float32)).astype(jnp.bfloat16)
    return jnp.dot(scaled.T, scaled, preferred_element_type=jnp.float32)
```

```python
import itertools

import jax
import jax.numpy as jnp
from jax import lax
from jax.experimental import pallas as pl
from jax.experimental.pallas import tpu as pltpu
from jax.sharding import Mesh
from jax.sharding import PartitionSpec as P

NAMES = ("zh", "c", "y", "x", "zl")
SIZES = (2, 2, 4, 4, 2)
CHUNKS = 4
VMEM = 56 * 1024 * 1024


def z_shift(value, step):
    return lax.ppermute(value, ("zh", "zl"), [(z, (z + step) % 4) for z in range(4)])


def ring_shift(value, step, ring):
    table = []
    for c, y, x in itertools.product(range(2), range(4), range(4)):
        if c == ring:
            to = (c, y, (x + step) % 4)
        else:
            to = (c, (y + step) % 4, x)
        table.append(((c * 4 + y) * 4 + x, (to[0] * 4 + to[1]) * 4 + to[2]))
    return lax.ppermute(value, ("c", "y", "x"), table)


def whole(shape):
    return pl.BlockSpec(shape, lambda: (0,) * len(shape))


def in_vmem(kernel, outs, *args):
    return pl.pallas_call(
        kernel,
        out_shape=outs,
        in_specs=[
            pl.BlockSpec(memory_space=pltpu.SMEM)
            if a.dtype == jnp.int32 else whole(a.shape)
            for a in args
        ],
        out_specs=jax.tree.map(lambda o: whole(o.shape), outs),
        compiler_params=pltpu.CompilerParams(vmem_limit_bytes=VMEM),
    )(*args)


def shape_of(rows, cols, dtype=jnp.bfloat16):
    return jax.ShapeDtypeStruct((rows, cols), dtype)


def split_rows(place, jacobian, root):
    rows, params = jacobian.shape
    quarter, wide, half = params // 4, params // 16, params // 32

    def kernel(place_ref, jac_ref, root_ref, *outs):
        scale = root_ref[...]
        z, c, a = place_ref[0], place_ref[1], place_ref[2]
        for n, step in enumerate((0, 1, 3, 2)):
            at = pl.multiple_of(lax.rem(z + step, 4) * quarter, quarter)
            piece = jac_ref[:, pl.ds(at, quarter)].astype(jnp.float32)
            outs[n][...] = (scale * piece).astype(jnp.bfloat16)
        for n, step in enumerate((0, 1, 3, 2)):
            block = lax.rem(a + step, 4)
            for j in range(4):
                first = jnp.where(c == 0, 4 * j + block, 4 * block + j) * 2
                for h in range(2):
                    own = jnp.where(c == 0, h, 1 - h)
                    at = pl.multiple_of((first + own) * half, half)
                    piece = jac_ref[:, pl.ds(at, half)].astype(jnp.float32)
                    outs[4 + n][:, j * wide + h * half : j * wide + (h + 1) * half] = (
                        scale * piece
                    ).astype(jnp.bfloat16)

    return in_vmem(kernel, [shape_of(rows, quarter)] * 8, place, jacobian, root)


def regroup_columns(place, pieces):
    rows, quarter = pieces[0].shape
    wide = quarter // 4

    def kernel(place_ref, *refs):
        b = place_ref[3]
        for n, step in enumerate((0, 1, 3, 2)):
            at = pl.multiple_of(lax.rem(b + step, 4) * wide, wide)
            for i in range(4):
                refs[4 + n][i * rows : (i + 1) * rows, :] = refs[i][:, pl.ds(at, wide)]

    return in_vmem(kernel, [shape_of(4 * rows, wide)] * 4, place, *pieces)


def stack_chunks(pieces, widths):
    rows = [p.shape[0] for p in pieces]

    def kernel(*refs):
        outs = refs[len(pieces) :]
        at = 0
        for out, width in zip(outs, widths):
            top = 0
            for piece, n in zip(refs, rows):
                out[top : top + n, :] = piece[:, at : at + width]
                top += n
            at += width

    return in_vmem(kernel, [shape_of(sum(rows), w) for w in widths], *pieces)


def products(pieces, columns):
    width, half = pieces[0].shape[1], columns.shape[1] // 2
    block = min(256, width)

    def kernel(*refs):
        rows = jnp.concatenate([r[...] for r in refs[: len(pieces)]], axis=0)
        total = lax.dot_general(
            rows, refs[len(pieces)][...], (((0,), (0,)), ((), ())), preferred_element_type=jnp.float32
        )
        refs[-2][...] = total[:, :half]
        refs[-1][...] = total[:, half:]

    return pl.pallas_call(
        kernel,
        grid=(width // block,),
        in_specs=[pl.BlockSpec((p.shape[0], block), lambda i: (0, i)) for p in pieces]
        + [pl.BlockSpec(columns.shape, lambda i: (0, 0))],
        out_specs=[pl.BlockSpec((block, half), lambda i: (i, 0))] * 2,
        out_shape=[shape_of(width, half, jnp.float32)] * 2,
        compiler_params=pltpu.CompilerParams(vmem_limit_bytes=VMEM),
    )(*pieces, columns)


def on_device(jacobian, obs_weights, time_to_obs):
    rows, params = jacobian.shape
    quarter, wide = params // 4, params // 16
    zh, c, y, x, zl = (lax.axis_index(n) for n in NAMES)
    a = jnp.where(c == 0, x, y)
    b = jnp.where(c == 0, y, x)
    place = jnp.stack([2 * zh + zl, c, a, b]).astype(jnp.int32)

    indices = jnp.arange(obs_weights.shape[0], dtype=jnp.int32)
    picked = jnp.sum(
        jnp.where(time_to_obs[:, None] == indices[None, :], obs_weights[None, :], 0.0), axis=1
    )
    cut = split_rows(place, jacobian, jnp.sqrt(picked)[:, None])

    first = [cut[4]] + [ring_shift(cut[4 + n], s, 0) for n, s in ((1, 1), (2, -1), (3, 2))]
    groups = regroup_columns(place, first)
    second = [groups[0]] + [ring_shift(groups[n], s, 1) for n, s in ((1, 1), (2, -1), (3, 2))]
    flat = jnp.concatenate(second, axis=0)
    back = z_shift(flat, 1)
    front = z_shift(flat, -1)
    mid = flat.shape[0] // 2
    far = [z_shift(back[:mid], 1), z_shift(front[mid:], -1)]
    columns = jnp.stack([flat, back, front, jnp.concatenate(far, axis=0)])
    columns = columns.reshape(4, 16, rows, wide).transpose(1, 0, 2, 3).reshape(64 * rows, wide)

    column = jnp.concatenate(
        [cut[0]] + [z_shift(cut[n], s) for n, s in ((1, 1), (2, -1), (3, 2))], axis=0
    )
    ring = [column] + [ring_shift(column, s, 0) for s in (1, -1, 2)]
    widths = [quarter // CHUNKS] * CHUNKS
    done = []
    for group in stack_chunks(ring, widths):
        back = ring_shift(group, 1, 1)
        front = ring_shift(group, -1, 1)
        mid = group.shape[0] // 2
        far = [ring_shift(back[:mid], 1, 1), ring_shift(front[mid:], -1, 1)]
        mine, other = products([group, back, front] + far, columns)
        mine = mine + lax.ppermute(other, "c", [(0, 1), (1, 0)])
        moved = lax.ppermute(mine.astype(jnp.bfloat16), ("c", "zl"), [(1, 2), (2, 1)])
        done.append(jnp.where(c == zl, mine, moved.astype(jnp.float32)))
    return jnp.concatenate(done, axis=0)


def solution(mesh):
    fine = Mesh(mesh.devices.reshape(SIZES), NAMES)
    rows = ("zh", "c", "y", "x", "zl")
    return jax.shard_map(
        on_device,
        mesh=fine,
        in_specs=(P(rows, None), P(), P(rows)),
        out_specs=P(("zh", "c"), ("y", "x", "zl")),
        check_vma=False,
    )
```

```python
import itertools

import jax
import jax.numpy as jnp
from jax import lax
from jax.experimental import pallas as pl
from jax.experimental.pallas import tpu as pltpu
from jax.sharding import Mesh
from jax.sharding import PartitionSpec as P

NAMES = ("zh", "c", "y", "x", "zl")
SIZES = (2, 2, 4, 4, 2)
CHUNKS = (4, 6, 4, 2)
SCOPED = 8 * 1024 * 1024


def z_shift(value, step):
    return lax.ppermute(value, ("zh", "zl"), [(z, (z + step) % 4) for z in range(4)])


def ring_shift(value, step, ring):
    table = []
    for c, y, x in itertools.product(range(2), range(4), range(4)):
        if c == ring:
            to = (c, y, (x + step) % 4)
        else:
            to = (c, (y + step) % 4, x)
        table.append(((c * 4 + y) * 4 + x, (to[0] * 4 + to[1]) * 4 + to[2]))
    return lax.ppermute(value, ("c", "y", "x"), table)


def in_vmem(kernel, outs, *args):
    return pl.pallas_call(
        kernel,
        out_shape=outs,
        in_specs=[
            pl.BlockSpec(memory_space=pltpu.SMEM if v.dtype == jnp.int32 else pltpu.VMEM)
            for v in args
        ],
        out_specs=[pl.BlockSpec(memory_space=pltpu.VMEM)] * len(outs),
        compiler_params=pltpu.CompilerParams(vmem_limit_bytes=SCOPED),
    )(*args)


def shape_of(rows, cols, dtype=jnp.bfloat16):
    return jax.ShapeDtypeStruct((rows, cols), dtype)


def split_rows(place, jacobian, root):
    rows, params = jacobian.shape
    quarter, wide, half = params // 4, params // 16, params // 32

    def kernel(place_ref, jac_ref, root_ref, *outs):
        scale = root_ref[...]
        z, c, a = place_ref[0], place_ref[1], place_ref[2]
        for n, step in enumerate((0, 1, 3, 2)):
            at = pl.multiple_of(lax.rem(z + step, 4) * quarter, quarter)
            piece = jac_ref[:, pl.ds(at, quarter)].astype(jnp.float32)
            outs[n][...] = (scale * piece).astype(jnp.bfloat16)
        for n, step in enumerate((0, 1, 3, 2)):
            block = lax.rem(a + step, 4)
            for j in range(4):
                first = jnp.where(c == 0, 4 * j + block, 4 * block + j) * 2
                for h in range(2):
                    own = jnp.where(c == 0, h, 1 - h)
                    at = pl.multiple_of((first + own) * half, half)
                    piece = jac_ref[:, pl.ds(at, half)].astype(jnp.float32)
                    outs[4 + n][:, j * wide + h * half : j * wide + (h + 1) * half] = (
                        scale * piece
                    ).astype(jnp.bfloat16)

    return in_vmem(kernel, [shape_of(rows, quarter)] * 8, place, jacobian, root)


def regroup_columns(place, pieces):
    rows, quarter = pieces[0].shape
    wide = quarter // 4

    def kernel(place_ref, *refs):
        b = place_ref[3]
        for n, step in enumerate((0, 1, 3, 2)):
            at = pl.multiple_of(lax.rem(b + step, 4) * wide, wide)
            for i in range(4):
                refs[4 + n][i * rows : (i + 1) * rows, :] = refs[i][:, pl.ds(at, wide)]

    return in_vmem(kernel, [shape_of(4 * rows, wide)] * 4, place, *pieces)


def stack_chunks(pieces, widths):
    rows = [p.shape[0] for p in pieces]

    def kernel(*refs):
        outs = refs[len(pieces) :]
        at = 0
        for out, width in zip(outs, widths):
            top = 0
            for piece, n in zip(refs, rows):
                out[top : top + n, :] = piece[:, at : at + width]
                top += n
            at += width

    return in_vmem(kernel, [shape_of(sum(rows), w) for w in widths], *pieces)


def products(pieces, columns):
    width, half = pieces[0].shape[1], columns.shape[1] // 2
    block = min(256, width)

    def kernel(*refs):
        mine, other = refs[-2:]
        right = refs[len(pieces)][...]
        for at in range(0, width, block):
            left = jnp.concatenate([r[:, at : at + block] for r in refs[: len(pieces)]], axis=0)
            total = lax.dot_general(
                left, right, (((0,), (0,)), ((), ())), preferred_element_type=jnp.float32
            )
            mine[at : at + block, :] = total[:, :half]
            other[at : at + block, :] = total[:, half:].astype(jnp.bfloat16)

    outs = [shape_of(width, half, jnp.float32), shape_of(width, half)]
    return in_vmem(kernel, outs, *pieces, columns)


def core_swap(value):
    return lax.ppermute(value, "c", [(0, 1), (1, 0)])


def write_out(out, total, at, stays, mine, moved):
    width, cols = mine.shape

    def kernel(stays_ref, mine_ref, moved_ref, *refs):
        out_ref, buffer, sem = refs[-3:]
        buffer[...] = jnp.where(stays_ref[0] == 1, mine_ref[...], moved_ref[...].astype(jnp.float32))
        copy = pltpu.make_async_copy(buffer, out_ref.at[pl.ds(at, width), :], sem)
        copy.start()
        copy.wait()

    args = [stays, mine, moved] + ([] if out is None else [out])
    return pl.pallas_call(
        kernel,
        out_shape=shape_of(total, cols, jnp.float32),
        in_specs=[pl.BlockSpec(memory_space=pltpu.SMEM)]
        + [pl.BlockSpec(memory_space=pltpu.VMEM)] * 2
        + ([] if out is None else [pl.BlockSpec(memory_space=pl.ANY)]),
        out_specs=pl.BlockSpec(memory_space=pl.ANY),
        scratch_shapes=[pltpu.VMEM((width, cols), jnp.float32), pltpu.SemaphoreType.DMA(())],
        input_output_aliases={} if out is None else {3: 0},
        compiler_params=pltpu.CompilerParams(vmem_limit_bytes=SCOPED),
    )(*args)


def on_device(jacobian, obs_weights, time_to_obs):
    rows, params = jacobian.shape
    quarter, wide = params // 4, params // 16
    zh, c, y, x, zl = (lax.axis_index(n) for n in NAMES)
    a = jnp.where(c == 0, x, y)
    b = jnp.where(c == 0, y, x)
    place = jnp.stack([2 * zh + zl, c, a, b]).astype(jnp.int32)

    indices = jnp.arange(obs_weights.shape[0], dtype=jnp.int32)
    picked = jnp.sum(
        jnp.where(time_to_obs[:, None] == indices[None, :], obs_weights[None, :], 0.0), axis=1
    )
    cut = split_rows(place, jacobian, jnp.sqrt(picked)[:, None])

    with jax.named_scope("columns_first"):
        first = [cut[4]] + [ring_shift(cut[4 + n], s, 0) for n, s in ((1, 1), (2, -1), (3, 2))]
        groups = regroup_columns(place, first)
    with jax.named_scope("columns_second"):
        second = [groups[0]] + [ring_shift(groups[n], s, 1) for n, s in ((1, 1), (2, -1), (3, 2))]
        flat = jnp.concatenate(second, axis=0)
    with jax.named_scope("columns_near"):
        back = z_shift(flat, 1)
        front = z_shift(flat, -1)
        columns_near = [back, front]
    mid = flat.shape[0] // 2
    with jax.named_scope("columns_far"):
        far = columns_far = [z_shift(back[:mid], 1), z_shift(front[mid:], -1)]
        columns = jnp.stack([flat, back, front, jnp.concatenate(far, axis=0)])
        columns = columns.reshape(4, 16, rows, wide).transpose(1, 0, 2, 3).reshape(64 * rows, wide)

    with jax.named_scope("panel_z"):
        column = jnp.concatenate(
            [cut[0]] + [z_shift(cut[n], s) for n, s in ((1, 1), (2, -1), (3, 2))], axis=0
        )
        column, _ = lax.optimization_barrier((column, flat))
    with jax.named_scope("panel_ring"):
        ring = [column] + [ring_shift(column, s, 0) for s in (1, -1, 2)]
    widths = [quarter // 16 * n for n in CHUNKS]
    near, far = [], []
    ring, _ = lax.optimization_barrier((ring, columns_near))
    for n, group in enumerate(stack_chunks(ring, widths)):
        if n > 1:
            group, _ = lax.optimization_barrier((group, far[n - 2]))
        with jax.named_scope(f"near{n}"):
            back = ring_shift(group, 1, 1)
            front = ring_shift(group, -1, 1)
        mid = group.shape[0] // 2
        near.append([group, back, front])
        before = far[n - 1] if n > 0 else columns_far
        (back, front), _ = lax.optimization_barrier(((back, front), before))
        with jax.named_scope(f"far{n}"):
            far.append([ring_shift(back[:mid], 1, 1), ring_shift(front[mid:], -1, 1)])
    sums, sent, last = [], [], len(widths) - 1
    for n in range(len(widths)):
        with jax.named_scope(f"product{n}"):
            mine, other = products(near[n] + far[n], columns)
        gate = []
        if n == 0:
            gate += near[1][1:]
        elif n < last:
            gate += far[n + 1]
        if 0 < n and n + 1 < last:
            gate += near[n + 2][1:]
        if n > 0:
            gate.append(sent[n - 1])
            gate.append(sums[max(n - 2, 0)][1])
        other, _ = lax.optimization_barrier((other, gate))
        with jax.named_scope(f"exchange{n}"):
            mine = mine + core_swap(other).astype(jnp.float32)
            sent.append(mine.astype(jnp.bfloat16))
        with jax.named_scope(f"swap{n}"):
            sums.append((mine, lax.ppermute(sent[n], ("c", "zl"), [(1, 2), (2, 1)])))
    stays = (c == zl).astype(jnp.int32).reshape(1)
    stays, _ = lax.optimization_barrier((stays, sent))
    out, at = None, 0
    for width, (mine, moved) in zip(widths, sums):
        out = write_out(out, quarter, at, stays, mine, moved)
        at += width
    return out


def solution(mesh):
    fine = Mesh(mesh.devices.reshape(SIZES), NAMES)
    rows = ("zh", "c", "y", "x", "zl")
    return jax.shard_map(
        on_device,
        mesh=fine,
        in_specs=(P(rows, None), P(), P(rows)),
        out_specs=P(("zh", "c"), ("y", "x", "zl")),
        check_vma=False,
    )
```

```python
import itertools

import jax
import jax.numpy as jnp
from jax import lax
from jax.experimental import pallas as pl
from jax.experimental.pallas import tpu as pltpu
from jax.sharding import Mesh
from jax.sharding import PartitionSpec as P

NAMES = ("zh", "c", "y", "x", "zl")
SIZES = (2, 2, 4, 4, 2)
CHUNKS = (4, 6, 4, 2)
SCOPED = 8 * 1024 * 1024


def z_shift(value, step):
    return lax.ppermute(value, ("zh", "zl"), [(z, (z + step) % 4) for z in range(4)])


def ring_shift(value, step, ring):
    table = []
    for c, y, x in itertools.product(range(2), range(4), range(4)):
        if c == ring:
            to = (c, y, (x + step) % 4)
        else:
            to = (c, (y + step) % 4, x)
        table.append(((c * 4 + y) * 4 + x, (to[0] * 4 + to[1]) * 4 + to[2]))
    return lax.ppermute(value, ("c", "y", "x"), table)


def in_vmem(kernel, outs, *args):
    return pl.pallas_call(
        kernel,
        out_shape=outs,
        in_specs=[
            pl.BlockSpec(memory_space=pltpu.SMEM if v.dtype == jnp.int32 else pltpu.VMEM)
            for v in args
        ],
        out_specs=[pl.BlockSpec(memory_space=pltpu.VMEM)] * len(outs),
        compiler_params=pltpu.CompilerParams(vmem_limit_bytes=SCOPED),
    )(*args)


def shape_of(rows, cols, dtype=jnp.bfloat16):
    return jax.ShapeDtypeStruct((rows, cols), dtype)


def split_rows(place, jacobian, root):
    rows, params = jacobian.shape
    quarter, wide, half = params // 4, params // 16, params // 32

    def kernel(place_ref, jac_ref, root_ref, *outs):
        scale = root_ref[...]
        z, c, a = place_ref[0], place_ref[1], place_ref[2]
        for n, step in enumerate((0, 1, 3, 2)):
            at = pl.multiple_of(lax.rem(z + step, 4) * quarter, quarter)
            piece = jac_ref[:, pl.ds(at, quarter)].astype(jnp.float32)
            outs[n][...] = (scale * piece).astype(jnp.bfloat16)
        for n, step in enumerate((0, 1, 3, 2)):
            block = lax.rem(a + step, 4)
            for j in range(4):
                first = jnp.where(c == 0, 4 * j + block, 4 * block + j) * 2
                for h in range(2):
                    own = jnp.where(c == 0, h, 1 - h)
                    at = pl.multiple_of((first + own) * half, half)
                    piece = jac_ref[:, pl.ds(at, half)].astype(jnp.float32)
                    outs[4 + n][:, j * wide + h * half : j * wide + (h + 1) * half] = (
                        scale * piece
                    ).astype(jnp.bfloat16)

    return in_vmem(kernel, [shape_of(rows, quarter)] * 8, place, jacobian, root)


def regroup_columns(place, pieces):
    rows, quarter = pieces[0].shape
    wide = quarter // 4

    def kernel(place_ref, *refs):
        b = place_ref[3]
        for n, step in enumerate((0, 1, 3, 2)):
            at = pl.multiple_of(lax.rem(b + step, 4) * wide, wide)
            for i in range(4):
                refs[4 + n][i * rows : (i + 1) * rows, :] = refs[i][:, pl.ds(at, wide)]

    return in_vmem(kernel, [shape_of(4 * rows, wide)] * 4, place, *pieces)


def stack_chunks(pieces, widths):
    rows = [p.shape[0] for p in pieces]

    def kernel(*refs):
        outs = refs[len(pieces) :]
        at = 0
        for out, width in zip(outs, widths):
            top = 0
            for piece, n in zip(refs, rows):
                out[top : top + n, :] = piece[:, at : at + width]
                top += n
            at += width

    return in_vmem(kernel, [shape_of(sum(rows), w) for w in widths], *pieces)


def products(pieces, columns):
    width, half = pieces[0].shape[1], columns.shape[1] // 2
    block = min(256, width)

    def kernel(*refs):
        mine, other = refs[-2:]
        right = refs[len(pieces)][...]
        for at in range(0, width, block):
            left = jnp.concatenate([r[:, at : at + block] for r in refs[: len(pieces)]], axis=0)
            total = lax.dot_general(
                left, right, (((0,), (0,)), ((), ())), preferred_element_type=jnp.float32
            )
            mine[at : at + block, :] = total[:, :half]
            other[at : at + block, :] = total[:, half:].astype(jnp.bfloat16)

    outs = [shape_of(width, half, jnp.float32), shape_of(width, half)]
    return in_vmem(kernel, outs, *pieces, columns)


def core_swap(value):
    return lax.ppermute(value, "c", [(0, 1), (1, 0)])


def write_out(out, total, at, stays, mine, moved):
    width, cols = mine.shape

    def kernel(stays_ref, mine_ref, moved_ref, *refs):
        out_ref, buffer, sem = refs[-3:]
        buffer[...] = jnp.where(stays_ref[0] == 1, mine_ref[...], moved_ref[...].astype(jnp.float32))
        copy = pltpu.make_async_copy(buffer, out_ref.at[pl.ds(at, width), :], sem)
        copy.start()
        copy.wait()

    args = [stays, mine, moved] + ([] if out is None else [out])
    return pl.pallas_call(
        kernel,
        out_shape=shape_of(total, cols, jnp.float32),
        in_specs=[pl.BlockSpec(memory_space=pltpu.SMEM)]
        + [pl.BlockSpec(memory_space=pltpu.VMEM)] * 2
        + ([] if out is None else [pl.BlockSpec(memory_space=pl.ANY)]),
        out_specs=pl.BlockSpec(memory_space=pl.ANY),
        scratch_shapes=[pltpu.VMEM((width, cols), jnp.float32), pltpu.SemaphoreType.DMA(())],
        input_output_aliases={} if out is None else {3: 0},
        compiler_params=pltpu.CompilerParams(vmem_limit_bytes=SCOPED),
    )(*args)


def on_device(jacobian, obs_weights, time_to_obs):
    rows, params = jacobian.shape
    quarter, wide = params // 4, params // 16
    zh, c, y, x, zl = (lax.axis_index(n) for n in NAMES)
    a = jnp.where(c == 0, x, y)
    b = jnp.where(c == 0, y, x)
    place = jnp.stack([2 * zh + zl, c, a, b]).astype(jnp.int32)

    indices = jnp.arange(obs_weights.shape[0], dtype=jnp.int32)
    picked = jnp.sum(
        jnp.where(time_to_obs[:, None] == indices[None, :], obs_weights[None, :], 0.0), axis=1
    )
    cut = split_rows(place, jacobian, jnp.sqrt(picked)[:, None])

    with jax.named_scope("columns_first"):
        first = [cut[4]] + [ring_shift(cut[4 + n], s, 0) for n, s in ((1, 1), (2, -1), (3, 2))]
        groups = regroup_columns(place, first)
    with jax.named_scope("columns_second"):
        second = [groups[0]] + [ring_shift(groups[n], s, 1) for n, s in ((1, 1), (2, -1), (3, 2))]
        flat = jnp.concatenate(second, axis=0)
    with jax.named_scope("columns_near"):
        back = z_shift(flat, 1)
        front = z_shift(flat, -1)
        columns_near = [back, front]
    mid = flat.shape[0] // 2
    with jax.named_scope("columns_far"):
        far = columns_far = [z_shift(back[:mid], 1), z_shift(front[mid:], -1)]
        columns = jnp.stack([flat, back, front, jnp.concatenate(far, axis=0)])
        columns = columns.reshape(4, 16, rows, wide).transpose(1, 0, 2, 3).reshape(64 * rows, wide)

    with jax.named_scope("panel_z"):
        column = jnp.concatenate(
            [cut[0]] + [z_shift(cut[n], s) for n, s in ((1, 1), (2, -1), (3, 2))], axis=0
        )
        column, _ = lax.optimization_barrier((column, flat))
    with jax.named_scope("panel_ring"):
        ring = [column] + [ring_shift(column, s, 0) for s in (1, -1, 2)]
    widths = [quarter // 16 * n for n in CHUNKS]
    near, far = [], []
    ring, _ = lax.optimization_barrier((ring, columns_near))
    for n, group in enumerate(stack_chunks(ring, widths)):
        if n > 1:
            group, _ = lax.optimization_barrier((group, far[n - 2]))
        with jax.named_scope(f"near{n}"):
            back = ring_shift(group, 1, 1)
            front = ring_shift(group, -1, 1)
        mid = group.shape[0] // 2
        near.append([group, back, front])
        before = far[n - 1] if n > 0 else columns_far
        (back, front), _ = lax.optimization_barrier(((back, front), before))
        with jax.named_scope(f"far{n}"):
            far.append([ring_shift(back[:mid], 1, 1), ring_shift(front[mid:], -1, 1)])
    sums, sent, last = [], [], len(widths) - 1
    for n in range(len(widths)):
        with jax.named_scope(f"product{n}"):
            mine, other = products(near[n] + far[n], columns)
        gate = []
        if n < last:
            gate += far[n + 1]
        if 0 < n and n + 1 < last:
            gate += near[n + 2][1:]
        if n > 0:
            gate.append(sent[n - 1])
        if n > 0:
            gate.append(sums[max(n - 2, 0)][1])
        if gate:
            other, _ = lax.optimization_barrier((other, gate))
        with jax.named_scope(f"exchange{n}"):
            mine = mine + core_swap(other).astype(jnp.float32)
            sent.append(mine.astype(jnp.bfloat16))
        with jax.named_scope(f"swap{n}"):
            sums.append((mine, lax.ppermute(sent[n], ("c", "zl"), [(1, 2), (2, 1)])))
    stays = (c == zl).astype(jnp.int32).reshape(1)
    stays, _ = lax.optimization_barrier((stays, sent))
    out, at = None, 0
    for width, (mine, moved) in zip(widths, sums):
        out = write_out(out, quarter, at, stays, mine, moved)
        at += width
    return out


def solution(mesh):
    fine = Mesh(mesh.devices.reshape(SIZES), NAMES)
    rows = ("zh", "c", "y", "x", "zl")
    return jax.shard_map(
        on_device,
        mesh=fine,
        in_specs=(P(rows, None), P(), P(rows)),
        out_specs=P(("zh", "c"), ("y", "x", "zl")),
        check_vma=False,
    )
```

```python
import itertools

import jax
import jax.numpy as jnp
from jax import lax
from jax.experimental import pallas as pl
from jax.experimental.pallas import tpu as pltpu
from jax.sharding import Mesh
from jax.sharding import PartitionSpec as P

NAMES = ("zh", "c", "y", "x", "zl")
SIZES = (2, 2, 4, 4, 2)
CHUNKS = (4, 6, 4, 2)
SCOPED = 8 * 1024 * 1024


def z_shift(value, step):
    return lax.ppermute(value, ("zh", "zl"), [(z, (z + step) % 4) for z in range(4)])


def ring_shift(value, step, ring):
    table = []
    for c, y, x in itertools.product(range(2), range(4), range(4)):
        if c == ring:
            to = (c, y, (x + step) % 4)
        else:
            to = (c, (y + step) % 4, x)
        table.append(((c * 4 + y) * 4 + x, (to[0] * 4 + to[1]) * 4 + to[2]))
    return lax.ppermute(value, ("c", "y", "x"), table)


def in_vmem(kernel, outs, *args):
    return pl.pallas_call(
        kernel,
        out_shape=outs,
        in_specs=[
            pl.BlockSpec(memory_space=pltpu.SMEM if v.dtype == jnp.int32 else pltpu.VMEM)
            for v in args
        ],
        out_specs=[pl.BlockSpec(memory_space=pltpu.VMEM)] * len(outs),
        compiler_params=pltpu.CompilerParams(vmem_limit_bytes=SCOPED),
    )(*args)


def shape_of(rows, cols, dtype=jnp.bfloat16):
    return jax.ShapeDtypeStruct((rows, cols), dtype)


def split_rows(place, jacobian, root):
    rows, params = jacobian.shape
    quarter, wide, half = params // 4, params // 16, params // 32

    def kernel(place_ref, jac_ref, root_ref, *outs):
        scale = root_ref[...]
        z, c, a = place_ref[0], place_ref[1], place_ref[2]
        for n, step in enumerate((0, 1, 3, 2)):
            at = pl.multiple_of(lax.rem(z + step, 4) * quarter, quarter)
            piece = jac_ref[:, pl.ds(at, quarter)].astype(jnp.float32)
            outs[n][...] = (scale * piece).astype(jnp.bfloat16)
        for n, step in enumerate((0, 1, 3, 2)):
            block = lax.rem(a + step, 4)
            for j in range(4):
                first = jnp.where(c == 0, 4 * j + block, 4 * block + j) * 2
                for h in range(2):
                    own = jnp.where(c == 0, h, 1 - h)
                    at = pl.multiple_of((first + own) * half, half)
                    piece = jac_ref[:, pl.ds(at, half)].astype(jnp.float32)
                    outs[4 + n][:, j * wide + h * half : j * wide + (h + 1) * half] = (
                        scale * piece
                    ).astype(jnp.bfloat16)

    return in_vmem(kernel, [shape_of(rows, quarter)] * 8, place, jacobian, root)


def regroup_columns(place, pieces):
    rows, quarter = pieces[0].shape
    wide = quarter // 4

    def kernel(place_ref, *refs):
        b = place_ref[3]
        for n, step in enumerate((0, 1, 3, 2)):
            at = pl.multiple_of(lax.rem(b + step, 4) * wide, wide)
            for i in range(4):
                refs[4 + n][i * rows : (i + 1) * rows, :] = refs[i][:, pl.ds(at, wide)]

    return in_vmem(kernel, [shape_of(4 * rows, wide)] * 4, place, *pieces)


def stack_chunks(pieces, widths):
    rows = [p.shape[0] for p in pieces]

    def kernel(*refs):
        outs = refs[len(pieces) :]
        at = 0
        for out, width in zip(outs, widths):
            top = 0
            for piece, n in zip(refs, rows):
                out[top : top + n, :] = piece[:, at : at + width]
                top += n
            at += width

    return in_vmem(kernel, [shape_of(sum(rows), w) for w in widths], *pieces)


def products(pieces, columns):
    width, half = pieces[0].shape[1], columns.shape[1] // 2
    block = min(256, width)

    def kernel(*refs):
        mine, other = refs[-2:]
        right = refs[len(pieces)][...]
        for at in range(0, width, block):
            left = jnp.concatenate([r[:, at : at + block] for r in refs[: len(pieces)]], axis=0)
            total = lax.dot_general(
                left, right, (((0,), (0,)), ((), ())), preferred_element_type=jnp.float32
            )
            mine[at : at + block, :] = total[:, :half]
            other[at : at + block, :] = total[:, half:].astype(jnp.bfloat16)

    outs = [shape_of(width, half, jnp.float32), shape_of(width, half)]
    return in_vmem(kernel, outs, *pieces, columns)


def core_swap(value):
    return lax.ppermute(value, "c", [(0, 1), (1, 0)])


def write_out(out, total, at, stays, mine, moved):
    width, cols = mine.shape

    def kernel(stays_ref, mine_ref, moved_ref, *refs):
        out_ref, buffer, sem = refs[-3:]
        buffer[...] = jnp.where(stays_ref[0] == 1, mine_ref[...], moved_ref[...].astype(jnp.float32))
        copy = pltpu.make_async_copy(buffer, out_ref.at[pl.ds(at, width), :], sem)
        copy.start()
        copy.wait()

    args = [stays, mine, moved] + ([] if out is None else [out])
    return pl.pallas_call(
        kernel,
        out_shape=shape_of(total, cols, jnp.float32),
        in_specs=[pl.BlockSpec(memory_space=pltpu.SMEM)]
        + [pl.BlockSpec(memory_space=pltpu.VMEM)] * 2
        + ([] if out is None else [pl.BlockSpec(memory_space=pl.ANY)]),
        out_specs=pl.BlockSpec(memory_space=pl.ANY),
        scratch_shapes=[pltpu.VMEM((width, cols), jnp.float32), pltpu.SemaphoreType.DMA(())],
        input_output_aliases={} if out is None else {3: 0},
        compiler_params=pltpu.CompilerParams(vmem_limit_bytes=SCOPED),
    )(*args)


def on_device(jacobian, obs_weights, time_to_obs):
    rows, params = jacobian.shape
    quarter, wide = params // 4, params // 16
    zh, c, y, x, zl = (lax.axis_index(n) for n in NAMES)
    a = jnp.where(c == 0, x, y)
    b = jnp.where(c == 0, y, x)
    place = jnp.stack([2 * zh + zl, c, a, b]).astype(jnp.int32)

    indices = jnp.arange(obs_weights.shape[0], dtype=jnp.int32)
    picked = jnp.sum(
        jnp.where(time_to_obs[:, None] == indices[None, :], obs_weights[None, :], 0.0), axis=1
    )
    cut = split_rows(place, jacobian, jnp.sqrt(picked)[:, None])

    with jax.named_scope("columns_first"):
        first = [cut[4]] + [ring_shift(cut[4 + n], s, 0) for n, s in ((1, 1), (2, -1), (3, 2))]
        groups = regroup_columns(place, first)
    with jax.named_scope("columns_second"):
        second = [groups[0]] + [ring_shift(groups[n], s, 1) for n, s in ((1, 1), (2, -1), (3, 2))]
        flat = jnp.concatenate(second, axis=0)
    with jax.named_scope("columns_near"):
        back = z_shift(flat, 1)
        front = z_shift(flat, -1)
        columns_near = [back, front]
    mid = flat.shape[0] // 2
    with jax.named_scope("columns_far"):
        far = columns_far = [z_shift(back[:mid], 1), z_shift(front[mid:], -1)]
        columns = jnp.stack([flat, back, front, jnp.concatenate(far, axis=0)])
        columns = columns.reshape(4, 16, rows, wide).transpose(1, 0, 2, 3).reshape(64 * rows, wide)

    with jax.named_scope("panel_z"):
        column = jnp.concatenate(
            [cut[0]] + [z_shift(cut[n], s) for n, s in ((1, 1), (2, -1), (3, 2))], axis=0
        )
        column, _ = lax.optimization_barrier((column, flat))
    with jax.named_scope("panel_ring"):
        ring = [column] + [ring_shift(column, s, 0) for s in (1, -1, 2)]
    widths = [quarter // 16 * n for n in CHUNKS]
    near, far = [], []
    ring, _ = lax.optimization_barrier((ring, columns_near))
    for n, group in enumerate(stack_chunks(ring, widths)):
        if n > 1:
            group, _ = lax.optimization_barrier((group, far[n - 2]))
        with jax.named_scope(f"near{n}"):
            back = ring_shift(group, 1, 1)
            front = ring_shift(group, -1, 1)
        mid = group.shape[0] // 2
        near.append([group, back, front])
        before = far[n - 1] if n > 0 else columns_far
        (back, front), _ = lax.optimization_barrier(((back, front), before))
        with jax.named_scope(f"far{n}"):
            far.append([ring_shift(back[:mid], 1, 1), ring_shift(front[mid:], -1, 1)])
    sums, sent, last = [], [], len(widths) - 1
    for n in range(len(widths)):
        with jax.named_scope(f"product{n}"):
            mine, other = products(near[n] + far[n], columns)
        gate = []
        if n < last:
            gate += far[n + 1]
        if 0 < n and n + 1 < last:
            gate += near[n + 2][1:]
        if n > 0:
            gate.append(sent[n - 1])
        if 0 < n < last:
            gate.append(sums[max(n - 2, 0)][1])
        if gate:
            other, _ = lax.optimization_barrier((other, gate))
        with jax.named_scope(f"exchange{n}"):
            mine = mine + core_swap(other).astype(jnp.float32)
            sent.append(mine.astype(jnp.bfloat16))
        if n == last:
            sent[n], _ = lax.optimization_barrier((sent[n], sums[n - 2][1]))
        with jax.named_scope(f"swap{n}"):
            sums.append((mine, lax.ppermute(sent[n], ("c", "zl"), [(1, 2), (2, 1)])))
    stays = (c == zl).astype(jnp.int32).reshape(1)
    stays, _ = lax.optimization_barrier((stays, sent))
    out, at = None, 0
    for width, (mine, moved) in zip(widths, sums):
        out = write_out(out, quarter, at, stays, mine, moved)
        at += width
    return out


def solution(mesh):
    fine = Mesh(mesh.devices.reshape(SIZES), NAMES)
    rows = ("zh", "c", "y", "x", "zl")
    return jax.shard_map(
        on_device,
        mesh=fine,
        in_specs=(P(rows, None), P(), P(rows)),
        out_specs=P(("zh", "c"), ("y", "x", "zl")),
        check_vma=False,
    )
```
